256 devices in a mesh: wide: 16 (over x, y_hi, core), narrow: 16 (over z, y_lo).
Axes of the slice: x: 4, y: 4 (y_hi: 2, y_lo: 2; y = y_hi * 2 + y_lo), z: 8, core: 2. Of those that a mesh axis runs over, the one named last changes fastest.
Arguments:
- entity_table: float32 [262144, 512], P(('wide', 'narrow')), may hold values from -1 to 1
- row_state: float32 [262144], P(('wide', 'narrow')), may hold values from 0.001 to 0.01
- operators: float32 [4, 512, 512], P(None, 'narrow'), may hold values from -0.25 to 0.25
- op_state: float32 [4, 512, 512], P(None, 'narrow', 'wide'), may hold values from 1 to 100
- head_index: int32 [2, 262144], P(None, ('wide', 'narrow')), may hold values from 0 to 1023
- tail_index: int32 [2, 262144], P(None, ('wide', 'narrow')), may hold values from 0 to 1023
- batch_relation: int32 [2, 1024], P(None, ('wide', 'narrow')), may hold values from 0 to 3
Outputs:
- new_table: float32 [262144, 512], P(('wide', 'narrow'))
- new_state: float32 [262144], P(('wide', 'narrow'))
- new_operators: float32 [4, 512, 512], P(None, 'narrow', 'wide')
- new_op_state: float32 [4, 512, 512], P(None, 'narrow', 'wide')
The draws below stay inside these ranges and needn't reach their ends.
Inputs may be any that keep to these rules, and one draw needn't show every extreme that they name: `head_index`: a row of the edge's head partition. `tail_index`: a row of the bucket's tail partition.
All inputs are finite; a program needn't handle non-finite values.
Results may differ from the reference program's by a relative error of at most 0.01.
Values may be sent and summed in bfloat16 or wider, within the bound.
No kernel may reach another device: no remote copies, remote signals or barrier semaphores. Data moves between devices by JAX's collectives and lax.ppermute only.
A program may use at most 64 MiB of HBM per device.

```python
import math
import jax
import jax.numpy as jnp
from jax import lax

D = 512
ENT = 1024
EDGES = 1024
BATCH = 256
NREL = 4
ENTITIES = 262144
EDGES_ALL = 262144
BATCHES_ALL = 1024
N_NARROW = 16
DEVICES = 256


def with_ends(entries, stream_key, smallest, top_value):
    spot = [jax.random.randint(jax.random.fold_in(stream_key, axis), (), 0, length) for axis, length in enumerate(entries.shape)]
    main_axis = entries.shape.index(max(entries.shape))
    beside = spot[:main_axis] + [(spot[main_axis] + 1) % entries.shape[main_axis]] + spot[main_axis + 1:]
    return entries.at[tuple(spot)].set(smallest).at[tuple(beside)].set(top_value)


def levels(own_key, extent, cuts, low, top_value):
    gain = 1.0
    for dim, blocks in cuts:
        draws = jax.random.uniform(jax.random.fold_in(jax.random.fold_in(own_key, 6), dim), (blocks,), jnp.float32, low / len(cuts), top_value / len(cuts))
        gain = gain * jnp.repeat(jnp.exp(draws), extent[dim] // blocks).reshape((-1,) + (1,) * (len(extent) - 1 - dim))
    return gain


def centred(stream_key, extent, width, reach, shards=(), held_as=jnp.bfloat16):
    gain = levels(stream_key, extent, shards, -0.22, 0.18) if shards else 1.0
    array = jax.random.normal(stream_key, extent, jnp.float32) * width * gain
    return jnp.minimum(jnp.maximum(array, -reach), reach).astype(held_as)


def setup_inputs(seed: int = 0) -> dict:
    keys = jax.random.split(jax.random.key(seed), 8)
    entity_table = centred(keys[0], (ENTITIES, D), 0.2, 1.0, ((0, 256),), jnp.float32)
    row_state = jnp.clip(jnp.exp(math.log(0.01) - 2.30258502 * jax.random.uniform(keys[1], (ENTITIES,), jnp.float32) ** levels(keys[1], (ENTITIES,), ((0, 256),), -0.2, 0.2)), 0.001, 0.01)
    operators = centred(keys[2], (NREL, D, D), D ** -0.5, 0.25, ((1, 16),), jnp.float32)
    op_state = jnp.clip(jnp.exp(math.log(100.0) - 4.6051702 * jax.random.uniform(keys[3], (NREL, D, D), jnp.float32) ** levels(keys[3], (NREL, D, D), ((1, 16), (2, 16)), -0.2, 0.2)), 1.0, 100.0)
    head_index = with_ends(jax.random.randint(keys[4], (2, EDGES_ALL), 0, ENT), jax.random.fold_in(keys[4], 1), 0, ENT - 1).astype(jnp.int32)
    tail_index = with_ends(jax.random.randint(keys[5], (2, EDGES_ALL), 0, ENT), jax.random.fold_in(keys[5], 1), 0, ENT - 1).astype(jnp.int32)
    batch_relation = with_ends(jax.random.randint(keys[6], (2, BATCHES_ALL), 0, NREL), jax.random.fold_in(keys[6], 1), 0, NREL - 1).astype(jnp.int32)
    return {"entity_table": entity_table, "row_state": row_state, "operators": operators, "op_state": op_state, "head_index": head_index, "tail_index": tail_index, "batch_relation": batch_relation}


LEARN_RATE = 0.1

def one_hot_rows(index, count):
    return (index[:, None] == jnp.arange(count, dtype=jnp.int32)[None, :]).astype(jnp.float32)

def bucket_terms(heads_bf, tails_bf, operators_bf, head_rows, tail_rows, relations):
    batches = relations.shape[0]
    picked = heads_bf[head_rows]
    blocked = picked.reshape(batches, -1, picked.shape[1])
    chosen = operators_bf[relations]
    query = jnp.einsum('bej,bij->bei', blocked.astype(jnp.float32), chosen.astype(jnp.float32)).astype(jnp.bfloat16)
    query_rows = query.reshape(picked.shape)
    scores = jnp.dot(query_rows, tails_bf.T, preferred_element_type=jnp.float32)
    weights = jnp.exp(scores)
    weights = weights / lax.optimization_barrier(jnp.sum(weights, axis=1, keepdims=True))
    score_grad = (weights - one_hot_rows(tail_rows, tails_bf.shape[0])).astype(jnp.bfloat16)
    query_grad = jnp.dot(score_grad, tails_bf, preferred_element_type=jnp.float32).astype(jnp.bfloat16)
    tail_grad = jnp.dot(score_grad.T, query_rows, preferred_element_type=jnp.float32).astype(jnp.bfloat16)
    grad_blocked = query_grad.reshape(query.shape).astype(jnp.float32)
    head_part = jnp.einsum('bei,bij->bej', grad_blocked, chosen.astype(jnp.float32)).reshape(picked.shape)
    head_grad = jnp.zeros(heads_bf.shape, jnp.float32).at[head_rows].add(head_part)
    per_batch = jnp.einsum('bei,bej->bij', grad_blocked, blocked.astype(jnp.float32))
    op_grad = jnp.einsum('br,bij->rij', one_hot_rows(relations, operators_bf.shape[0]), per_batch)
    return (head_grad, tail_grad, op_grad)

def reference(entity_table, row_state, operators, op_state, head_index, tail_index, batch_relation):
    table_bf = entity_table.reshape(DEVICES, ENT, D).astype(jnp.bfloat16)
    operators_bf = operators.astype(jnp.bfloat16)
    heads = head_index.reshape(2, DEVICES, EDGES)
    tails = tail_index.reshape(2, DEVICES, EDGES)
    relations = batch_relation.reshape(2, DEVICES, EDGES // BATCH)
    flips = (1, N_NARROW // 2)

    def visit(op_sum, device):
        head_sum = jnp.zeros((ENT, D), jnp.float32)
        tail_list = []
        for bucket in range(2):
            partner = jnp.bitwise_xor(device, flips[bucket])
            head_grad, tail_grad, op_grad = bucket_terms(table_bf[device], table_bf[partner], operators_bf, heads[bucket, device], tails[bucket, device], relations[bucket, device])
            head_sum = head_sum + head_grad
            tail_list.append(tail_grad)
            op_sum = op_sum + op_grad
        return (op_sum, (head_sum, jnp.stack(tail_list)))
    devices_all = jnp.arange(DEVICES, dtype=jnp.int32)
    op_total, (head_all, tail_all) = lax.scan(visit, jnp.zeros((NREL, D, D), jnp.float32), devices_all)
    back_first = tail_all[jnp.bitwise_xor(devices_all, flips[0]), 0].astype(jnp.float32)
    back_second = tail_all[jnp.bitwise_xor(devices_all, flips[1]), 1].astype(jnp.float32)
    entity_grad = (head_all + back_first + back_second).reshape(ENTITIES, D)
    new_state = row_state + lax.optimization_barrier(jnp.mean(entity_grad * entity_grad, axis=1))
    new_table = entity_table - LEARN_RATE * entity_grad / jnp.sqrt(new_state)[:, None]
    new_op_state = op_state + op_total * op_total
    new_operators = operators - LEARN_RATE * op_total / jnp.sqrt(new_op_state)
    return (new_table, new_state, new_operators, new_op_state)
```

```python
import jax
import jax.numpy as jnp
from jax import lax
from jax.sharding import PartitionSpec as P

LEARN_RATE = 0.1


def swapped(block, axis, stride):
    count = lax.axis_size(axis)
    return lax.ppermute(block, axis, [(i, i ^ (1 << stride)) for i in range(count)])


def picks(index, count, dtype):
    return (index[:, None] == jnp.arange(count, dtype=jnp.int32)[None, :]).astype(dtype)


def spread(piece, axis):
    count = lax.axis_size(axis)
    return lax.all_to_all(jnp.broadcast_to(piece[None], (count, *piece.shape)), axis, 0, 0)


def whole_operators(operators):
    nrel, rows, width = operators.shape
    wide, narrow = lax.axis_size("wide"), lax.axis_size("narrow")
    pieces = operators.astype(jnp.bfloat16).reshape(wide, nrel * rows // wide, width)
    own = lax.dynamic_index_in_dim(pieces, lax.axis_index("wide"), 0, keepdims=False)
    across = spread(spread(own, "narrow"), "wide")
    split = across.reshape(nrel, wide // nrel, narrow, -1, width)
    return split.transpose(0, 2, 1, 3, 4).reshape(nrel, rows * narrow, width)


def bucket_terms(heads_bf, tails_bf, operators_bf, head_rows, tail_rows, relations):
    batches = relations.shape[0]
    chosen_rows = picks(head_rows, heads_bf.shape[0], jnp.bfloat16)
    picked = jnp.dot(chosen_rows, heads_bf, preferred_element_type=jnp.bfloat16)
    blocked = picked.reshape(batches, -1, picked.shape[1])
    chosen = operators_bf[relations]
    query = jnp.einsum("bej,bij->bei", blocked, chosen, preferred_element_type=jnp.float32).astype(
        jnp.bfloat16
    )
    query_rows = query.reshape(picked.shape)
    scores = jnp.einsum("ed,td->et", query_rows, tails_bf, preferred_element_type=jnp.float32)
    weights = jnp.exp(scores)
    weights = weights / jnp.sum(weights, axis=1, keepdims=True)
    target = picks(tail_rows, tails_bf.shape[0], jnp.float32)
    score_grad = (weights - target).astype(jnp.bfloat16)
    tail_grad = jnp.einsum(
        "et,ed->td", score_grad, query_rows, preferred_element_type=jnp.float32
    ).astype(jnp.bfloat16)
    query_grad = jnp.dot(score_grad, tails_bf, preferred_element_type=jnp.float32).astype(
        jnp.bfloat16
    )
    grad_blocked = query_grad.reshape(query.shape)
    head_part = jnp.einsum(
        "bei,bij->bej", grad_blocked, chosen, preferred_element_type=jnp.float32
    ).reshape(picked.shape)
    head_grad = jnp.einsum(
        "et,ed->td",
        chosen_rows,
        head_part.astype(jnp.bfloat16),
        preferred_element_type=jnp.float32,
    )
    per_batch = jnp.einsum(
        "bej,bei->bji", blocked, grad_blocked, preferred_element_type=jnp.float32
    )
    op_grad = jnp.einsum("br,bji->rji", picks(relations, operators_bf.shape[0], jnp.float32), per_batch)
    return (head_grad, tail_grad, op_grad)


def reduced_op_grad(op_total):
    nrel, width, _ = op_total.shape
    wide, narrow = lax.axis_size("wide"), lax.axis_size("narrow")
    sent = op_total.astype(jnp.bfloat16).reshape(nrel, wide, width // wide, width)
    got = lax.all_to_all(sent.transpose(1, 0, 2, 3), "wide", 0, 0)
    part = jnp.sum(got.astype(jnp.float32), axis=0).reshape(-1, width).T
    part = part.astype(jnp.bfloat16).reshape(narrow, width // narrow, part.shape[1])
    got = lax.all_to_all(part, "narrow", 0, 0)
    total = jnp.sum(got.astype(jnp.float32), axis=0)
    return total.reshape(width // narrow, nrel, width // wide).transpose(1, 0, 2)


def body(entity_table, row_state, operators, op_state, head_index, tail_index, batch_relation):
    narrow_count = lax.axis_size("narrow")
    wide_count = lax.axis_size("wide")
    table_bf = entity_table.astype(jnp.bfloat16)
    top_bit = narrow_count.bit_length() - 2
    flips = (0, top_bit)
    tails = [None, None]
    for bucket in (1, 0):
        tails[bucket] = swapped(table_bf, "narrow", flips[bucket])
    operators_bf = whole_operators(operators)
    head_total = jnp.zeros(entity_table.shape, jnp.float32)
    op_total = jnp.zeros(operators_bf.shape, jnp.float32)
    returned = [None, None]
    for bucket in (1, 0):
        head_grad, tail_grad, op_grad = bucket_terms(
            table_bf,
            tails[bucket],
            operators_bf,
            head_index[bucket],
            tail_index[bucket],
            batch_relation[bucket],
        )
        head_total = head_total + head_grad
        op_total = op_total + op_grad
        returned[bucket] = swapped(tail_grad, "narrow", flips[bucket])
    op_shard = reduced_op_grad(op_total)
    entity_grad = head_total + returned[0].astype(jnp.float32) + returned[1].astype(jnp.float32)
    new_state = row_state + jnp.mean(entity_grad * entity_grad, axis=1)
    new_table = entity_table - LEARN_RATE * entity_grad / jnp.sqrt(new_state)[:, None]
    columns = operators.shape[2] // wide_count
    first_column = lax.axis_index("wide") * columns
    own_operators = lax.dynamic_slice_in_dim(operators, first_column, columns, 2)
    new_op_state = op_state + op_shard * op_shard
    new_operators = own_operators - LEARN_RATE * op_shard / jnp.sqrt(new_op_state)
    return (new_table, new_state, new_operators, new_op_state)


def solution(mesh):
    placed = (
        P(("wide", "narrow"), None),
        P(("wide", "narrow")),
        P(None, "narrow", None),
        P(None, "narrow", "wide"),
        P(None, ("wide", "narrow")),
        P(None, ("wide", "narrow")),
        P(None, ("wide", "narrow")),
    )
    return jax.shard_map(
        body,
        mesh=mesh,
        in_specs=placed,
        out_specs=(
            P(("wide", "narrow"), None),
            P(("wide", "narrow")),
            P(None, "narrow", "wide"),
            P(None, "narrow", "wide"),
        ),
        check_vma=False,
    )
```

```python
import jax
import jax.numpy as jnp
from jax import lax
from jax.experimental import pallas as pl
from jax.experimental.pallas import tpu as pltpu
from jax.sharding import PartitionSpec as P


LEARN_RATE = 0.1
BF = jnp.bfloat16
F32 = jnp.float32
NN = (((1,), (0,)), ((), ()))
NT = (((1,), (1,)), ((), ()))
TN = (((0,), (0,)), ((), ()))


def dot(a, b, dims):
    return lax.dot_general(a, b, dims, preferred_element_type=F32)


def swapped(block, axis, stride):
    count = lax.axis_size(axis)
    return lax.ppermute(block, axis, [(i, i ^ (1 << stride)) for i in range(count)])


def same_core():
    return [list(range(core, lax.axis_size("wide"), 2)) for core in range(2)]


def spread(piece, count, axis, groups=None):
    sent = jnp.broadcast_to(piece[None], (count, *piece.shape))
    return lax.all_to_all(sent, axis, 0, 0, axis_index_groups=groups)


def whole_operators(operators):
    nrel, rows, width = operators.shape
    chips, narrow = lax.axis_size("wide") // 2, lax.axis_size("narrow")
    place = lax.axis_index("wide")
    chip, core = place // 2, place % 2
    high, half = nrel * rows // chips, width // 2
    pieces = operators.astype(BF).reshape(chips, high, width)
    own = lax.dynamic_index_in_dim(pieces, chip, 0, keepdims=False)
    own = lax.dynamic_slice_in_dim(own, core * half, half, 1)
    across = spread(own, narrow, "narrow")
    across = spread(across, chips, "wide", same_core())
    other = swapped(across, "wide", 0)
    first = jnp.where(core == 0, across, other)
    second = jnp.where(core == 0, other, across)
    full = jnp.concatenate([first, second], axis=-1)
    full = full.reshape(nrel, chips // nrel, narrow, high, width)
    return full.transpose(0, 2, 1, 3, 4).reshape(nrel, rows * narrow, width)


def forward_kernel(relations, heads, tails, operators, head_at, tail_at, rows, query_grad, tail_grad, total):
    batches = relations.shape[0]
    edges = rows.shape[0] // batches
    count = tails.shape[0]

    def one(batch, carry):
        at = pl.ds(pl.multiple_of(batch * edges, edges), edges)
        lane = lax.broadcasted_iota(jnp.int32, (edges, count), 1)
        picks = (head_at[at, :] == lane).astype(F32).astype(BF)
        row = dot(picks, heads[...], NN).astype(BF)
        rows[at, :] = row
        query = dot(row, operators[relations[batch]], NT).astype(BF)
        weights = jnp.exp(dot(query, tails[...], NT))
        weights = weights * (1.0 / jnp.sum(weights, axis=1, keepdims=True))
        grad = (weights - (tail_at[at, :] == lane).astype(F32)).astype(BF)
        part = dot(grad, query, TN)

        @pl.when(batch == 0)
        def _():
            total[...] = part

        @pl.when(batch > 0)
        def _():
            total[...] += part

        query_grad[at, :] = dot(grad, tails[...], NN).astype(BF)
        return carry

    lax.fori_loop(0, batches, one, 0)
    tail_grad[...] = total[...].astype(BF)


def vmem():
    return pl.BlockSpec(memory_space=pltpu.VMEM)


def smem():
    return pl.BlockSpec(memory_space=pltpu.SMEM)


def forward(heads, tails, operators, head_at, tail_at, relations):
    edges, (count, width) = head_at.shape[0], heads.shape
    return pl.pallas_call(
        forward_kernel,
        out_shape=(
            jax.ShapeDtypeStruct((edges, width), BF),
            jax.ShapeDtypeStruct((edges, width), BF),
            jax.ShapeDtypeStruct((count, width), BF),
        ),
        in_specs=[smem()] + [vmem()] * 5,
        out_specs=(vmem(), vmem(), vmem()),
        scratch_shapes=[pltpu.VMEM((count, width), F32)],
        cost_estimate=pl.CostEstimate(
            flops=9 * edges * count * width, bytes_accessed=16 * count * width, transcendentals=edges * count
        ),
        name="forward",
    )(relations, heads, tails, operators, head_at, tail_at)


def operator_kernel(relations, core, rows0, grad0, rows1, grad1, kept, sent, total):
    batches = relations.shape[1]
    edges = rows0.shape[0] // batches
    width = rows0.shape[1]
    nrel, chips, _, columns, _ = total.shape
    total[...] = jnp.zeros_like(total)
    for bucket, (rows, grad) in enumerate(((rows0, grad0), (rows1, grad1))):

        def one(batch, carry, bucket=bucket, rows=rows, grad=grad):
            at = pl.ds(pl.multiple_of(batch * edges, edges), edges)
            part = dot(rows[at, :], grad[at, :], TN)
            total[relations[bucket, batch]] += part.reshape(chips, 2, columns, width)
            return carry

        lax.fori_loop(0, batches, one, 0)
    for r in range(nrel):
        kept[:, r] = total[r, :, core[0]]
        sent[:, r] = total[r, :, 1 - core[0]].astype(BF)


def operator_grad(relations, core, rows, grads, nrel, wide):
    edges, width = rows[0].shape
    shape = (wide // 2, nrel, width // wide, width)
    return pl.pallas_call(
        operator_kernel,
        out_shape=(jax.ShapeDtypeStruct(shape, F32), jax.ShapeDtypeStruct(shape, BF)),
        in_specs=[smem(), smem()] + [vmem()] * 4,
        out_specs=(vmem(), vmem()),
        scratch_shapes=[pltpu.VMEM((nrel, wide // 2, 2, width // wide, width), F32)],
        cost_estimate=pl.CostEstimate(
            flops=4 * edges * width * width, bytes_accessed=20 * edges * width, transcendentals=0
        ),
        name="operator_grad",
    )(relations, core, rows[0], grads[0], rows[1], grads[1])


def head_kernel(relations, head_at, grad0, grad1, operators, total):
    batches = relations.shape[1]
    edges = grad0.shape[0] // batches
    count = total.shape[0]
    for bucket, grad in enumerate((grad0, grad1)):
        for batch in range(batches):
            at = slice(batch * edges, (batch + 1) * edges)
            part = dot(grad[at, :], operators[relations[bucket, batch]], NN).astype(BF)
            row = lax.broadcasted_iota(jnp.int32, (count, edges), 0)
            picks = (head_at[bucket : bucket + 1, at] == row).astype(F32).astype(BF)
            added = dot(picks, part, NN)
            if bucket == 0 and batch == 0:
                total[...] = added
            else:
                total[...] += added


def head_grad(relations, head_at, grads, operators):
    edges, width = grads[0].shape
    return pl.pallas_call(
        head_kernel,
        out_shape=jax.ShapeDtypeStruct((edges, width), F32),
        in_specs=[smem()] + [vmem()] * 4,
        out_specs=vmem(),
        cost_estimate=pl.CostEstimate(
            flops=6 * edges * edges * width, bytes_accessed=12 * edges * width, transcendentals=0
        ),
        name="head_grad",
    )(relations, head_at, grads[0], grads[1], operators)


def summed_over_devices(kept, sent):
    _, nrel, columns, width = kept.shape
    narrow = lax.axis_size("narrow")
    pair = (kept + swapped(sent, "wide", 0).astype(F32)).astype(BF)
    got = lax.all_to_all(pair, "wide", 0, 0, axis_index_groups=same_core())
    part = jnp.sum(got.astype(F32), axis=0).reshape(nrel * columns, width).T
    got = lax.all_to_all(part.reshape(narrow, width // narrow, nrel * columns), "narrow", 0, 0)
    total = jnp.sum(got, axis=0)
    return total.reshape(width // narrow, nrel, columns).transpose(1, 0, 2)


def step(entity_table, row_state, operators, op_state, head_index, tail_index, batch_relation):
    narrow_count = lax.axis_size("narrow")
    wide_count = lax.axis_size("wide")
    flips = (0, narrow_count.bit_length() - 2)
    table_bf = entity_table.astype(BF)
    tails = [None, None]
    for bucket in (1, 0):
        tails[bucket] = swapped(table_bf, "narrow", flips[bucket])
    operators_bf = whole_operators(operators)
    rows, query_grads, returned = [None, None], [None, None], [None, None]
    for bucket in (0, 1):
        rows[bucket], query_grads[bucket], tail_grad = forward(
            table_bf,
            tails[bucket],
            operators_bf,
            head_index[bucket][:, None],
            tail_index[bucket][:, None],
            batch_relation[bucket],
        )
        returned[bucket] = swapped(tail_grad, "narrow", flips[bucket])
    core = (lax.axis_index("wide") % 2).astype(jnp.int32).reshape(1)
    kept, sent = operator_grad(batch_relation, core, rows, query_grads, operators.shape[0], wide_count)
    op_shard = summed_over_devices(kept, sent)
    head_total = head_grad(batch_relation, head_index, query_grads, operators_bf)
    entity_grad = head_total + returned[0].astype(F32) + returned[1].astype(F32)
    new_state = row_state + jnp.mean(entity_grad * entity_grad, axis=1)
    new_table = entity_table - LEARN_RATE * entity_grad / jnp.sqrt(new_state)[:, None]
    columns = operators.shape[2] // wide_count
    first_column = lax.axis_index("wide") * columns
    own_operators = lax.dynamic_slice_in_dim(operators, first_column, columns, 2)
    new_op_state = op_state + op_shard * op_shard
    new_operators = own_operators - LEARN_RATE * op_shard / jnp.sqrt(new_op_state)
    return (new_table, new_state, new_operators, new_op_state)


def solution(mesh):
    placed = (
        P(("wide", "narrow"), None),
        P(("wide", "narrow")),
        P(None, "narrow", None),
        P(None, "narrow", "wide"),
        P(None, ("wide", "narrow")),
        P(None, ("wide", "narrow")),
        P(None, ("wide", "narrow")),
    )
    return jax.shard_map(
        step,
        mesh=mesh,
        in_specs=placed,
        out_specs=(
            P(("wide", "narrow"), None),
            P(("wide", "narrow")),
            P(None, "narrow", "wide"),
            P(None, "narrow", "wide"),
        ),
        check_vma=False,
    )
```

```python
import jax
import jax.numpy as jnp
from jax import lax
from jax.experimental import pallas as pl
from jax.experimental.pallas import tpu as pltpu
from jax.sharding import PartitionSpec as P


LEARN_RATE = 0.1
BF = jnp.bfloat16
F32 = jnp.float32
NN = (((1,), (0,)), ((), ()))
NT = (((1,), (1,)), ((), ()))
TN = (((0,), (0,)), ((), ()))
VMEM_BYTES = 24 << 20


def dot(a, b, dims):
    return lax.dot_general(a, b, dims, preferred_element_type=F32)


def vmem(count):
    return [pl.BlockSpec(memory_space=pltpu.VMEM)] * count


def smem(count):
    return [pl.BlockSpec(memory_space=pltpu.SMEM)] * count


def local(kernel, flops, outs, scalars, arrays, scratch=()):
    shapes = tuple(jax.ShapeDtypeStruct(*out) for out in outs)
    moved = sum(a.size * a.dtype.itemsize for a in (*arrays, *shapes))
    return pl.pallas_call(
        kernel,
        out_shape=shapes,
        in_specs=smem(len(scalars)) + vmem(len(arrays)),
        out_specs=tuple(vmem(len(shapes))),
        scratch_shapes=list(scratch),
        compiler_params=pltpu.CompilerParams(vmem_limit_bytes=VMEM_BYTES),
        cost_estimate=pl.CostEstimate(flops=flops, bytes_accessed=moved, transcendentals=0),
    )(*scalars, *arrays)


def swapped(block, axis, stride):
    count = lax.axis_size(axis)
    return lax.ppermute(block, axis, [(i, i ^ (1 << stride)) for i in range(count)])


def strided_groups(size, stride):
    return [list(range(first, size, stride)) for first in range(stride)]


def spread(piece, count, axis, groups=None):
    sent = jnp.broadcast_to(piece[None], (count, *piece.shape))
    return lax.all_to_all(sent, axis, 0, 0, axis_index_groups=groups)


def own_half_of_operators(operators):
    nrel, rows, width = operators.shape
    wide, narrow = lax.axis_size("wide"), lax.axis_size("narrow")
    place, half = lax.axis_index("wide"), width // 2
    stride = wide // nrel
    own = lax.dynamic_index_in_dim(operators, place // stride, 0, keepdims=False)
    own = lax.dynamic_slice_in_dim(own, place % 2 * half, half, 1).astype(BF)
    across = spread(own, narrow, "narrow")
    across = spread(across, nrel, "wide", strided_groups(wide, stride))
    return across.reshape(nrel, narrow * rows, half)


def picks(index, first, rows):
    spot = lax.broadcasted_iota(jnp.int32, (rows, index.shape[1]), 0) + first
    return (index == spot).astype(F32).astype(BF)


def rows_kernel(head_at, heads, rows0, rows1):
    for bucket, rows in enumerate((rows0, rows1)):
        chosen = picks(head_at[bucket : bucket + 1, :], 0, heads.shape[0])
        rows[...] = dot(chosen, heads[...], TN).astype(BF)


def halves(core, half):
    own = pl.ds(pl.multiple_of(core * half, half), half)
    other = pl.ds(pl.multiple_of((1 - core) * half, half), half)
    return own, other


def query_kernel(relations, core, rows, own, other, query):
    batches = relations.shape[0]
    edges = rows.shape[0] // batches
    first, second = halves(core[0], own.shape[2])
    for batch in range(batches):
        at = slice(batch * edges, (batch + 1) * edges)
        r = relations[batch]
        found = dot(rows[at, first], own[r], NT) + dot(rows[at, second], other[r], NT)
        query[at, :] = found.astype(BF)


def score_kernel(query, tails, tail_at, score_grad, tail_grad):
    count, edges = tails.shape[0], query.shape[0]
    parts = 4
    step = edges // parts
    for part in range(parts):
        at = slice(part * step, (part + 1) * step)
        weights = jnp.exp(dot(tails[...], query[at, :], NT))
        weights = weights * (1.0 / jnp.sum(weights, axis=0, keepdims=True))
        hit = tail_at[:, at] == lax.broadcasted_iota(jnp.int32, (count, step), 0)
        score_grad[:, at] = jnp.where(hit, weights - 1.0, weights).astype(BF)
    tail_grad[...] = dot(score_grad[...], query[...], NN).astype(BF)


def query_grad_and_sum(relations, score_grad, tails, rows, query_grad, total):
    batches = relations.shape[0]
    edges = rows.shape[0] // batches
    query_grad[...] = dot(score_grad[...], tails[...], TN).astype(BF)
    for batch in range(batches):
        at = slice(batch * edges, (batch + 1) * edges)
        part = dot(rows[at, :], query_grad[at, :], TN)
        total[relations[batch]] += part.reshape(total.shape[1:])


def first_backward_kernel(relations, score_grad, tails, rows, query_grad, total):
    total[...] = jnp.zeros_like(total)
    query_grad_and_sum(relations, score_grad, tails, rows, query_grad, total)


def last_backward_kernel(relations, core, score_grad, tails, rows, before, query_grad, kept, sent, total):
    total[...] = before[...]
    query_grad_and_sum(relations, score_grad, tails, rows, query_grad, total)
    for r in range(total.shape[0]):
        kept[:, r] = total[r, :, core[0]]
        sent[:, r] = total[r, :, 1 - core[0]].astype(BF)


def head_kernel(relations, core, head_at, grad0, grad1, own, other, total, part):
    batches = relations.shape[1]
    edges = grad0.shape[0] // batches
    parts = 4
    step = total.shape[0] // parts
    first, second = halves(core[0], own.shape[2])
    for bucket, grad in enumerate((grad0, grad1)):
        for batch in range(batches):
            at = slice(batch * edges, (batch + 1) * edges)
            r = relations[bucket, batch]
            part[at, first] = dot(grad[at, :], own[r], NN).astype(BF)
            part[at, second] = dot(grad[at, :], other[r], NN).astype(BF)
        for k in range(parts):
            to = slice(k * step, (k + 1) * step)
            added = dot(picks(head_at[bucket : bucket + 1, :], k * step, step), part[...], NN)
            if bucket == 0:
                total[to, :] = added
            else:
                total[to, :] += added


def summed_over_devices(kept, sent):
    _, nrel, columns, width = kept.shape
    narrow = lax.axis_size("narrow")
    pair = (kept + swapped(sent, "wide", 0).astype(F32)).astype(BF)
    groups = strided_groups(lax.axis_size("wide"), 2)
    got = lax.all_to_all(pair, "wide", 0, 0, axis_index_groups=groups)
    part = jnp.sum(got.astype(F32), axis=0).reshape(nrel * columns, width).T
    got = lax.all_to_all(part.reshape(narrow, width // narrow, nrel * columns), "narrow", 0, 0)
    total = jnp.sum(got, axis=0)
    return total.reshape(width // narrow, nrel, columns).transpose(1, 0, 2)


def step(entity_table, row_state, operators, op_state, head_index, tail_index, batch_relation):
    nrel, _, width = operators.shape
    count, edges = entity_table.shape[0], head_index.shape[1]
    narrow_count = lax.axis_size("narrow")
    wide_count = lax.axis_size("wide")
    flips = (0, narrow_count.bit_length() - 2)
    core = (lax.axis_index("wide") % 2).astype(jnp.int32).reshape(1)
    table_bf = entity_table.astype(BF)
    half = own_half_of_operators(operators)
    tails = [None, None]
    for bucket in (1, 0):
        tails[bucket] = swapped(table_bf, "narrow", flips[bucket])
    other = swapped(half, "wide", 0)
    flat = ((edges, width), BF)
    matmul = 2 * count * edges * width
    rows = local(rows_kernel, 2 * matmul, (flat, flat), (), (head_index, table_bf))
    score_grads, returned, query_grads = [None, None], [None, None], [None, None]
    for bucket in (0, 1):
        (query,) = local(
            query_kernel,
            matmul // 2,
            (flat,),
            (batch_relation[bucket], core),
            (rows[bucket], half, other),
        )
        score_grads[bucket], tail_grad = local(
            score_kernel,
            4 * matmul,
            (((count, edges), BF), ((count, width), BF)),
            (),
            (query, tails[bucket], tail_index[bucket : bucket + 1]),
        )
        returned[bucket] = swapped(tail_grad, "narrow", flips[bucket])
    sums = (nrel, wide_count // 2, 2, width // wide_count, width)
    query_grads[0], before = local(
        first_backward_kernel,
        2 * matmul,
        (flat, (sums, F32)),
        (batch_relation[0],),
        (score_grads[0], tails[0], rows[0]),
    )
    shares = (wide_count // 2, nrel, width // wide_count, width)
    query_grads[1], kept, sent = local(
        last_backward_kernel,
        2 * matmul,
        (flat, (shares, F32), (shares, BF)),
        (batch_relation[1], core),
        (score_grads[1], tails[1], rows[1], before),
        (pltpu.VMEM(sums, F32),),
    )
    op_shard = summed_over_devices(kept, sent)
    (head_total,) = local(
        head_kernel,
        3 * matmul,
        (((count, width), F32),),
        (batch_relation, core),
        (head_index, *query_grads, half, other),
        (pltpu.VMEM((edges, width), BF),),
    )
    entity_grad = head_total + returned[0].astype(F32) + returned[1].astype(F32)
    new_state = row_state + jnp.mean(entity_grad * entity_grad, axis=1)
    new_table = entity_table - LEARN_RATE * entity_grad / jnp.sqrt(new_state)[:, None]
    columns = width // wide_count
    first_column = lax.axis_index("wide") * columns
    own_operators = lax.dynamic_slice_in_dim(operators, first_column, columns, 2)
    new_op_state = op_state + op_shard * op_shard
    new_operators = own_operators - LEARN_RATE * op_shard / jnp.sqrt(new_op_state)
    return (new_table, new_state, new_operators, new_op_state)


def solution(mesh):
    placed = (
        P(("wide", "narrow"), None),
        P(("wide", "narrow")),
        P(None, "narrow", None),
        P(None, "narrow", "wide"),
        P(None, ("wide", "narrow")),
        P(None, ("wide", "narrow")),
        P(None, ("wide", "narrow")),
    )
    return jax.shard_map(
        step,
        mesh=mesh,
        in_specs=placed,
        out_specs=(
            P(("wide", "narrow"), None),
            P(("wide", "narrow")),
            P(None, "narrow", "wide"),
            P(None, "narrow", "wide"),
        ),
        check_vma=False,
    )
```

```python
import jax
import jax.numpy as jnp
from jax import lax
from jax.experimental import pallas as pl
from jax.experimental.pallas import tpu as pltpu
from jax.sharding import PartitionSpec as P


LEARN_RATE = 0.1
BF = jnp.bfloat16
F32 = jnp.float32
NN = (((1,), (0,)), ((), ()))
NT = (((1,), (1,)), ((), ()))
TN = (((0,), (0,)), ((), ()))
VMEM_BYTES = 24 << 20


def dot(a, b, dims):
    return lax.dot_general(a, b, dims, preferred_element_type=F32)


def vmem(count):
    return [pl.BlockSpec(memory_space=pltpu.VMEM)] * count


def smem(count):
    return [pl.BlockSpec(memory_space=pltpu.SMEM)] * count


def local(kernel, flops, outs, scalars, arrays, scratch=()):
    shapes = tuple(jax.ShapeDtypeStruct(*out) for out in outs)
    moved = sum(a.size * a.dtype.itemsize for a in (*arrays, *shapes))
    return pl.pallas_call(
        kernel,
        out_shape=shapes,
        in_specs=smem(len(scalars)) + vmem(len(arrays)),
        out_specs=tuple(vmem(len(shapes))),
        scratch_shapes=list(scratch),
        compiler_params=pltpu.CompilerParams(vmem_limit_bytes=VMEM_BYTES),
        cost_estimate=pl.CostEstimate(flops=flops, bytes_accessed=moved, transcendentals=0),
    )(*scalars, *arrays)


def swapped(block, axis, stride):
    count = lax.axis_size(axis)
    return lax.ppermute(block, axis, [(i, i ^ (1 << stride)) for i in range(count)])


def strided_groups(size, stride):
    return [list(range(first, size, stride)) for first in range(stride)]


def spread(piece, count, axis, groups=None):
    sent = jnp.broadcast_to(piece[None], (count, *piece.shape))
    return lax.all_to_all(sent, axis, 0, 0, axis_index_groups=groups)


def own_half_of_operators(operators):
    nrel, rows, width = operators.shape
    wide, narrow = lax.axis_size("wide"), lax.axis_size("narrow")
    place, half = lax.axis_index("wide"), width // 2
    stride = wide // nrel
    own = lax.dynamic_index_in_dim(operators, place // stride, 0, keepdims=False)
    own = lax.dynamic_slice_in_dim(own, place % 2 * half, half, 1).astype(BF)
    across = spread(own, narrow, "narrow")
    across = spread(across, nrel, "wide", strided_groups(wide, stride))
    return across.reshape(nrel, narrow * rows, half)


def picks(index, first, rows):
    spot = lax.broadcasted_iota(jnp.int32, (rows, index.shape[1]), 0) + first
    return (index == spot).astype(F32).astype(BF)


def rows_kernel(head_at, heads, rows0, rows1):
    for bucket, rows in enumerate((rows0, rows1)):
        chosen = picks(head_at[bucket : bucket + 1, :], 0, heads.shape[0])
        rows[...] = dot(chosen, heads[...], TN).astype(BF)


def halves(core, half):
    own = pl.ds(pl.multiple_of(core * half, half), half)
    other = pl.ds(pl.multiple_of((1 - core) * half, half), half)
    return own, other


def query_kernel(relations, core, rows, own, other, query):
    batches = relations.shape[0]
    edges = rows.shape[0] // batches
    first, second = halves(core[0], own.shape[2])
    for batch in range(batches):
        at = slice(batch * edges, (batch + 1) * edges)
        r = relations[batch]
        found = dot(rows[at, first], own[r], NT) + dot(rows[at, second], other[r], NT)
        query[at, :] = found.astype(BF)


def score_kernel(query, tails, tail_at, score_grad, tail_grad):
    count, edges = tails.shape[0], query.shape[0]
    parts = 4
    step = edges // parts
    for part in range(parts):
        at = slice(part * step, (part + 1) * step)
        weights = jnp.exp(dot(tails[...], query[at, :], NT))
        weights = weights * (1.0 / jnp.sum(weights, axis=0, keepdims=True))
        hit = tail_at[:, at] == lax.broadcasted_iota(jnp.int32, (count, step), 0)
        score_grad[:, at] = jnp.where(hit, weights - 1.0, weights).astype(BF)
    tail_grad[...] = dot(score_grad[...], query[...], NN).astype(BF)


def query_grad_and_sum(relations, score_grad, tails, rows, query_grad, total):
    batches = relations.shape[0]
    edges = rows.shape[0] // batches
    query_grad[...] = dot(score_grad[...], tails[...], TN).astype(BF)
    for batch in range(batches):
        at = slice(batch * edges, (batch + 1) * edges)
        part = dot(rows[at, :], query_grad[at, :], TN)
        total[relations[batch]] += part.reshape(total.shape[1:])


def first_backward_kernel(relations, score_grad, tails, rows, query_grad, total):
    total[...] = jnp.zeros_like(total)
    query_grad_and_sum(relations, score_grad, tails, rows, query_grad, total)


def last_backward_kernel(relations, core, score_grad, tails, rows, before, query_grad, kept, sent, total):
    total[...] = before[...]
    query_grad_and_sum(relations, score_grad, tails, rows, query_grad, total)
    for r in range(total.shape[0]):
        kept[:, r] = total[r, :, core[0]]
        sent[:, r] = total[r, :, 1 - core[0]].astype(BF)


def head_kernel(relations, core, head_at, grad0, grad1, own, other, total, part):
    batches = relations.shape[1]
    edges = grad0.shape[0] // batches
    parts = 4
    step = total.shape[0] // parts
    first, second = halves(core[0], own.shape[2])
    for bucket, grad in enumerate((grad0, grad1)):
        for batch in range(batches):
            at = slice(batch * edges, (batch + 1) * edges)
            r = relations[bucket, batch]
            part[at, first] = dot(grad[at, :], own[r], NN).astype(BF)
            part[at, second] = dot(grad[at, :], other[r], NN).astype(BF)
        for k in range(parts):
            to = slice(k * step, (k + 1) * step)
            added = dot(picks(head_at[bucket : bucket + 1, :], k * step, step), part[...], NN)
            if bucket == 0:
                total[to, :] = added
            else:
                total[to, :] += added


def op_update_kernel(got, state, operators, new_operators, new_state):
    total = got[0].astype(F32)
    for source in range(1, got.shape[0]):
        total += got[source].astype(F32)
    columns = state.shape[2]
    for r in range(state.shape[0]):
        grad = total[:, r * columns : (r + 1) * columns]
        sums = state[r] + grad * grad
        new_state[r] = sums
        new_operators[r] = operators[r] - LEARN_RATE * grad / jnp.sqrt(sums)


def summed_over_devices(kept, sent):
    _, nrel, columns, width = kept.shape
    narrow = lax.axis_size("narrow")
    pair = (kept + swapped(sent, "wide", 0).astype(F32)).astype(BF)
    groups = strided_groups(lax.axis_size("wide"), 2)
    got = lax.all_to_all(pair, "wide", 0, 0, axis_index_groups=groups)
    part = jnp.sum(got.astype(F32), axis=0).reshape(nrel * columns, width).T
    part = part.astype(BF).reshape(narrow, width // narrow, nrel * columns)
    return lax.all_to_all(part, "narrow", 0, 0)


def step(entity_table, row_state, operators, op_state, head_index, tail_index, batch_relation):
    nrel, _, width = operators.shape
    count, edges = entity_table.shape[0], head_index.shape[1]
    narrow_count = lax.axis_size("narrow")
    wide_count = lax.axis_size("wide")
    flips = (0, narrow_count.bit_length() - 2)
    core = (lax.axis_index("wide") % 2).astype(jnp.int32).reshape(1)
    table_bf = entity_table.astype(BF)
    half = own_half_of_operators(operators)
    tails = [None, None]
    for bucket in (1, 0):
        tails[bucket] = swapped(table_bf, "narrow", flips[bucket])
    other = swapped(half, "wide", 0)
    flat = ((edges, width), BF)
    matmul = 2 * count * edges * width
    rows = local(rows_kernel, 2 * matmul, (flat, flat), (), (head_index, table_bf))
    score_grads, returned, query_grads = [None, None], [None, None], [None, None]
    for bucket in (0, 1):
        (query,) = local(
            query_kernel,
            matmul // 2,
            (flat,),
            (batch_relation[bucket], core),
            (rows[bucket], half, other),
        )
        score_grads[bucket], tail_grad = local(
            score_kernel,
            4 * matmul,
            (((count, edges), BF), ((count, width), BF)),
            (),
            (query, tails[bucket], tail_index[bucket : bucket + 1]),
        )
        returned[bucket] = swapped(tail_grad, "narrow", flips[bucket])
    sums = (nrel, wide_count // 2, 2, width // wide_count, width)
    query_grads[0], before = local(
        first_backward_kernel,
        2 * matmul,
        (flat, (sums, F32)),
        (batch_relation[0],),
        (score_grads[0], tails[0], rows[0]),
    )
    shares = (wide_count // 2, nrel, width // wide_count, width)
    query_grads[1], kept, sent = local(
        last_backward_kernel,
        2 * matmul,
        (flat, (shares, F32), (shares, BF)),
        (batch_relation[1], core),
        (score_grads[1], tails[1], rows[1], before),
        (pltpu.VMEM(sums, F32),),
    )
    op_parts = summed_over_devices(kept, sent)
    (head_total,) = local(
        head_kernel,
        3 * matmul,
        (((count, width), F32),),
        (batch_relation, core),
        (head_index, *query_grads, half, other),
        (pltpu.VMEM((edges, width), BF),),
    )
    entity_grad = head_total + returned[0].astype(F32) + returned[1].astype(F32)
    new_state = row_state + jnp.mean(entity_grad * entity_grad, axis=1)
    new_table = entity_table - LEARN_RATE * entity_grad / jnp.sqrt(new_state)[:, None]
    columns = width // wide_count
    first_column = lax.axis_index("wide") * columns
    own_operators = lax.dynamic_slice_in_dim(operators, first_column, columns, 2)
    share = (op_state.shape, F32)
    new_operators, new_op_state = local(
        op_update_kernel, 8 * op_state.size, (share, share), (), (op_parts, op_state, own_operators)
    )
    return (new_table, new_state, new_operators, new_op_state)


def solution(mesh):
    placed = (
        P(("wide", "narrow"), None),
        P(("wide", "narrow")),
        P(None, "narrow", None),
        P(None, "narrow", "wide"),
        P(None, ("wide", "narrow")),
        P(None, ("wide", "narrow")),
        P(None, ("wide", "narrow")),
    )
    return jax.shard_map(
        step,
        mesh=mesh,
        in_specs=placed,
        out_specs=(
            P(("wide", "narrow"), None),
            P(("wide", "narrow")),
            P(None, "narrow", "wide"),
            P(None, "narrow", "wide"),
        ),
        check_vma=False,
    )
```

```python
import jax
import jax.numpy as jnp
from jax import lax
from jax.experimental import pallas as pl
from jax.experimental.pallas import tpu as pltpu
from jax.sharding import PartitionSpec as P


LEARN_RATE = 0.1
BF = jnp.bfloat16
F32 = jnp.float32
NN = (((1,), (0,)), ((), ()))
NT = (((1,), (1,)), ((), ()))
TN = (((0,), (0,)), ((), ()))
VMEM_BYTES = 24 << 20
UPDATE_PARTS = 4


def dot(a, b, dims):
    return lax.dot_general(a, b, dims, preferred_element_type=F32)


def vmem(count):
    return [pl.BlockSpec(memory_space=pltpu.VMEM)] * count


def smem(count):
    return [pl.BlockSpec(memory_space=pltpu.SMEM)] * count


def local(kernel, flops, outs, scalars, arrays, scratch=()):
    shapes = tuple(jax.ShapeDtypeStruct(*out) for out in outs)
    moved = sum(a.size * a.dtype.itemsize for a in (*arrays, *shapes))
    return pl.pallas_call(
        kernel,
        out_shape=shapes,
        in_specs=smem(len(scalars)) + vmem(len(arrays)),
        out_specs=tuple(vmem(len(shapes))),
        scratch_shapes=list(scratch),
        compiler_params=pltpu.CompilerParams(vmem_limit_bytes=VMEM_BYTES),
        cost_estimate=pl.CostEstimate(flops=flops, bytes_accessed=moved, transcendentals=0),
    )(*scalars, *arrays)


def swapped(block, axis, stride):
    count = lax.axis_size(axis)
    return lax.ppermute(block, axis, [(i, i ^ (1 << stride)) for i in range(count)])


def strided_groups(size, stride):
    return [list(range(first, size, stride)) for first in range(stride)]


def spread(piece, count, axis, groups=None):
    sent = jnp.broadcast_to(piece[None], (count, *piece.shape))
    return lax.all_to_all(sent, axis, 0, 0, axis_index_groups=groups)


def own_half_of_operators(operators):
    nrel, rows, width = operators.shape
    wide, narrow = lax.axis_size("wide"), lax.axis_size("narrow")
    place, half = lax.axis_index("wide"), width // 2
    stride = wide // nrel
    own = lax.dynamic_index_in_dim(operators, place // stride, 0, keepdims=False)
    own = lax.dynamic_slice_in_dim(own, place % 2 * half, half, 1).astype(BF)
    across = spread(own, narrow, "narrow")
    across = spread(across, nrel, "wide", strided_groups(wide, stride))
    return across.reshape(nrel, narrow * rows, half)


def picks(index, first, rows):
    spot = lax.broadcasted_iota(jnp.int32, (rows, index.shape[1]), 0) + first
    return (index == spot).astype(F32).astype(BF)


def rows_kernel(head_at, heads, rows0, rows1):
    for bucket, rows in enumerate((rows0, rows1)):
        chosen = picks(head_at[bucket : bucket + 1, :], 0, heads.shape[0])
        rows[...] = dot(chosen, heads[...], TN).astype(BF)


def halves(core, half):
    own = pl.ds(pl.multiple_of(core * half, half), half)
    other = pl.ds(pl.multiple_of((1 - core) * half, half), half)
    return own, other


def query_kernel(relations, core, rows, own, other, query):
    batches = relations.shape[0]
    edges = rows.shape[0] // batches
    first, second = halves(core[0], own.shape[2])
    for batch in range(batches):
        at = slice(batch * edges, (batch + 1) * edges)
        r = relations[batch]
        found = dot(rows[at, first], own[r], NT) + dot(rows[at, second], other[r], NT)
        query[at, :] = found.astype(BF)


def score_kernel(query, tails, tail_at, score_grad, tail_grad):
    count, edges = tails.shape[0], query.shape[0]
    parts = 4
    step = edges // parts
    for part in range(parts):
        at = slice(part * step, (part + 1) * step)
        weights = jnp.exp(dot(tails[...], query[at, :], NT))
        weights = weights * (1.0 / jnp.sum(weights, axis=0, keepdims=True))
        hit = tail_at[:, at] == lax.broadcasted_iota(jnp.int32, (count, step), 0)
        score_grad[:, at] = jnp.where(hit, weights - 1.0, weights).astype(BF)
    tail_grad[...] = dot(score_grad[...], query[...], NN).astype(BF)


def query_grad_and_sum(relations, score_grad, tails, rows, query_grad, total):
    batches = relations.shape[0]
    edges = rows.shape[0] // batches
    query_grad[...] = dot(score_grad[...], tails[...], TN).astype(BF)
    for batch in range(batches):
        at = slice(batch * edges, (batch + 1) * edges)
        part = dot(rows[at, :], query_grad[at, :], TN)
        total[relations[batch]] += part.reshape(total.shape[1:])


def first_backward_kernel(relations, score_grad, tails, rows, query_grad, total):
    total[...] = jnp.zeros_like(total)
    query_grad_and_sum(relations, score_grad, tails, rows, query_grad, total)


def last_backward_kernel(relations, core, score_grad, tails, rows, before, query_grad, kept, sent, total):
    total[...] = before[...]
    query_grad_and_sum(relations, score_grad, tails, rows, query_grad, total)
    for r in range(total.shape[0]):
        kept[:, r] = total[r, :, core[0]]
        sent[:, r] = total[r, :, 1 - core[0]].astype(BF)


def head_kernel(relations, core, head_at, grad0, grad1, own, other, near, total, part):
    batches = relations.shape[1]
    edges = grad0.shape[0] // batches
    parts = 4
    step = total.shape[0] // parts
    first, second = halves(core[0], own.shape[2])
    for bucket, grad in enumerate((grad0, grad1)):
        for batch in range(batches):
            at = slice(batch * edges, (batch + 1) * edges)
            r = relations[bucket, batch]
            part[at, first] = dot(grad[at, :], own[r], NN).astype(BF)
            part[at, second] = dot(grad[at, :], other[r], NN).astype(BF)
        for k in range(parts):
            to = slice(k * step, (k + 1) * step)
            added = dot(picks(head_at[bucket : bucket + 1, :], k * step, step), part[...], NN)
            if bucket == 0:
                total[to, :] = added + near[to, :].astype(F32)
            else:
                total[to, :] += added


def update_kernel(far, head, table, state, new_table, new_state, held, into, out, out_done):
    parts, block = into.shape[0], state.shape[1]
    step = table.shape[0] // parts
    spans = [pl.ds(part * step, step) for part in range(parts)]
    coming = [pltpu.make_async_copy(far.at[to], held.at[to], into.at[part]) for part, to in enumerate(spans)]
    leaving = [pltpu.make_async_copy(out.at[to], new_table.at[to], out_done.at[part]) for part, to in enumerate(spans)]
    for copy in coming:
        copy.start()
    for part in range(parts):
        coming[part].wait()
        for first in range(part * step, (part + 1) * step, block):
            at, row = slice(first, first + block), slice(first // block, first // block + 1)
            grad = head[at, :] + held[at, :].astype(F32)
            before = jnp.broadcast_to(state[row, :], (block, block)).T[:, :1]
            sums = before + jnp.mean(grad * grad, axis=1, keepdims=True)
            new_state[row, :] = jnp.broadcast_to(sums, (block, block)).T[:1, :]
            out[at, :] = table[at, :] - grad * (LEARN_RATE / jnp.sqrt(sums))
        leaving[part].start()
    for copy in leaving:
        copy.wait()


def updated(head, far, table, state):
    count, width = table.shape
    block, parts = 128, UPDATE_PARTS
    anywhere = pl.BlockSpec(memory_space=pl.ANY)
    new_table, new_state = pl.pallas_call(
        update_kernel,
        out_shape=(
            jax.ShapeDtypeStruct(table.shape, F32),
            jax.ShapeDtypeStruct((count // block, block), F32),
        ),
        in_specs=[anywhere] + vmem(3),
        out_specs=(anywhere, vmem(1)[0]),
        scratch_shapes=[
            pltpu.VMEM((count, width), BF),
            pltpu.SemaphoreType.DMA((parts,)),
            pltpu.VMEM((count, width), F32),
            pltpu.SemaphoreType.DMA((parts,)),
        ],
        compiler_params=pltpu.CompilerParams(vmem_limit_bytes=VMEM_BYTES),
        cost_estimate=pl.CostEstimate(flops=8 * table.size, bytes_accessed=16 * table.size, transcendentals=0),
        name="update",
    )(far, head, table, state.reshape(count // block, block))
    return new_table, new_state.reshape(count)


def op_update_kernel(got, state, operators, new_operators, new_state):
    total = got[0].astype(F32)
    for source in range(1, got.shape[0]):
        total += got[source].astype(F32)
    columns = state.shape[2]
    for r in range(state.shape[0]):
        grad = total[:, r * columns : (r + 1) * columns]
        sums = state[r] + grad * grad
        new_state[r] = sums
        new_operators[r] = operators[r] - LEARN_RATE * grad / jnp.sqrt(sums)


def summed_over_devices(kept, sent):
    _, nrel, columns, width = kept.shape
    narrow = lax.axis_size("narrow")
    pair = (kept + swapped(sent, "wide", 0).astype(F32)).astype(BF)
    groups = strided_groups(lax.axis_size("wide"), 2)
    got = lax.all_to_all(pair, "wide", 0, 0, axis_index_groups=groups)
    part = jnp.sum(got.astype(F32), axis=0).reshape(nrel * columns, width).T
    part = part.astype(BF).reshape(narrow, width // narrow, nrel * columns)
    return lax.all_to_all(part, "narrow", 0, 0)


def step(entity_table, row_state, operators, op_state, head_index, tail_index, batch_relation):
    nrel, _, width = operators.shape
    count, edges = entity_table.shape[0], head_index.shape[1]
    narrow_count = lax.axis_size("narrow")
    wide_count = lax.axis_size("wide")
    flips = (0, narrow_count.bit_length() - 2)
    core = (lax.axis_index("wide") % 2).astype(jnp.int32).reshape(1)
    table_bf = entity_table.astype(BF)
    half = own_half_of_operators(operators)
    tails = [None, None]
    for bucket in (1, 0):
        tails[bucket] = swapped(table_bf, "narrow", flips[bucket])
    other = swapped(half, "wide", 0)
    flat = ((edges, width), BF)
    matmul = 2 * count * edges * width
    rows = local(rows_kernel, 2 * matmul, (flat, flat), (), (head_index, table_bf))
    score_grads, returned, query_grads = [None, None], [None, None], [None, None]
    for bucket in (0, 1):
        (query,) = local(
            query_kernel,
            matmul // 2,
            (flat,),
            (batch_relation[bucket], core),
            (rows[bucket], half, other),
        )
        score_grads[bucket], tail_grad = local(
            score_kernel,
            4 * matmul,
            (((count, edges), BF), ((count, width), BF)),
            (),
            (query, tails[bucket], tail_index[bucket : bucket + 1]),
        )
        returned[bucket] = swapped(tail_grad, "narrow", flips[bucket])
    sums = (nrel, wide_count // 2, 2, width // wide_count, width)
    query_grads[0], before = local(
        first_backward_kernel,
        2 * matmul,
        (flat, (sums, F32)),
        (batch_relation[0],),
        (score_grads[0], tails[0], rows[0]),
    )
    shares = (wide_count // 2, nrel, width // wide_count, width)
    query_grads[1], kept, sent = local(
        last_backward_kernel,
        2 * matmul,
        (flat, (shares, F32), (shares, BF)),
        (batch_relation[1], core),
        (score_grads[1], tails[1], rows[1], before),
        (pltpu.VMEM(sums, F32),),
    )
    op_parts = summed_over_devices(kept, sent)
    (head_total,) = local(
        head_kernel,
        3 * matmul,
        (((count, width), F32),),
        (batch_relation, core),
        (head_index, *query_grads, half, other, returned[0]),
        (pltpu.VMEM((edges, width), BF),),
    )
    new_table, new_state = updated(head_total, returned[1], entity_table, row_state)
    columns = width // wide_count
    first_column = lax.axis_index("wide") * columns
    own_operators = lax.dynamic_slice_in_dim(operators, first_column, columns, 2)
    share = (op_state.shape, F32)
    new_operators, new_op_state = local(
        op_update_kernel, 8 * op_state.size, (share, share), (), (op_parts, op_state, own_operators)
    )
    return (new_table, new_state, new_operators, new_op_state)


def solution(mesh):
    placed = (
        P(("wide", "narrow"), None),
        P(("wide", "narrow")),
        P(None, "narrow", None),
        P(None, "narrow", "wide"),
        P(None, ("wide", "narrow")),
        P(None, ("wide", "narrow")),
        P(None, ("wide", "narrow")),
    )
    return jax.shard_map(
        step,
        mesh=mesh,
        in_specs=placed,
        out_specs=(
            P(("wide", "narrow"), None),
            P(("wide", "narrow")),
            P(None, "narrow", "wide"),
            P(None, "narrow", "wide"),
        ),
        check_vma=False,
    )
```

```python
import jax
import jax.numpy as jnp
from jax import lax
from jax.experimental import pallas as pl
from jax.experimental.pallas import tpu as pltpu
from jax.sharding import PartitionSpec as P


LEARN_RATE = 0.1
BF = jnp.bfloat16
F32 = jnp.float32
NN = (((1,), (0,)), ((), ()))
NT = (((1,), (1,)), ((), ()))
TN = (((0,), (0,)), ((), ()))
VMEM_BYTES = 24 << 20
UPDATE_PARTS = 8


def dot(a, b, dims):
    return lax.dot_general(a, b, dims, preferred_element_type=F32)


def vmem(count):
    return [pl.BlockSpec(memory_space=pltpu.VMEM)] * count


def smem(count):
    return [pl.BlockSpec(memory_space=pltpu.SMEM)] * count


def local(kernel, flops, outs, scalars, arrays, scratch=()):
    shapes = tuple(jax.ShapeDtypeStruct(*out) for out in outs)
    moved = sum(a.size * a.dtype.itemsize for a in (*arrays, *shapes))
    return pl.pallas_call(
        kernel,
        out_shape=shapes,
        in_specs=smem(len(scalars)) + vmem(len(arrays)),
        out_specs=tuple(vmem(len(shapes))),
        scratch_shapes=list(scratch),
        compiler_params=pltpu.CompilerParams(vmem_limit_bytes=VMEM_BYTES),
        cost_estimate=pl.CostEstimate(flops=flops, bytes_accessed=moved, transcendentals=0),
    )(*scalars, *arrays)


def swapped(block, axis, stride):
    count = lax.axis_size(axis)
    return lax.ppermute(block, axis, [(i, i ^ (1 << stride)) for i in range(count)])


def strided_groups(size, stride):
    return [list(range(first, size, stride)) for first in range(stride)]


def spread(piece, count, axis, groups=None):
    sent = jnp.broadcast_to(piece[None], (count, *piece.shape))
    return lax.all_to_all(sent, axis, 0, 0, axis_index_groups=groups)


def own_half_of_operators(operators):
    nrel, rows, width = operators.shape
    wide, narrow = lax.axis_size("wide"), lax.axis_size("narrow")
    place, half = lax.axis_index("wide"), width // 2
    stride = wide // nrel
    own = lax.dynamic_index_in_dim(operators, place // stride, 0, keepdims=False)
    own = lax.dynamic_slice_in_dim(own, place % 2 * half, half, 1).astype(BF)
    across = spread(own, narrow, "narrow")
    across = spread(across, nrel, "wide", strided_groups(wide, stride))
    return across.reshape(nrel, narrow * rows, half)


def picks(index, first, rows):
    spot = lax.broadcasted_iota(jnp.int32, (rows, index.shape[1]), 0) + first
    return (index == spot).astype(F32).astype(BF)


def rows_kernel(head_at, heads, rows0, rows1):
    for bucket, rows in enumerate((rows0, rows1)):
        chosen = picks(head_at[bucket : bucket + 1, :], 0, heads.shape[0])
        rows[...] = dot(chosen, heads[...], TN).astype(BF)


def halves(core, half):
    own = pl.ds(pl.multiple_of(core * half, half), half)
    other = pl.ds(pl.multiple_of((1 - core) * half, half), half)
    return own, other


def query_kernel(relations, core, rows, own, other, query):
    batches = relations.shape[0]
    edges = rows.shape[0] // batches
    first, second = halves(core[0], own.shape[2])
    for batch in range(batches):
        at = slice(batch * edges, (batch + 1) * edges)
        r = relations[batch]
        found = dot(rows[at, first], own[r], NT) + dot(rows[at, second], other[r], NT)
        query[at, :] = found.astype(BF)


def score_kernel(query, tails, tail_at, score_grad, tail_grad):
    count, edges = tails.shape[0], query.shape[0]
    step, block = edges // 4, count // 4
    for part in range(4):
        at = slice(part * step, (part + 1) * step)
        weights = [jnp.exp(dot(tails[k * block : (k + 1) * block, :], query[at, :], NT)) for k in range(4)]
        scale = 1.0 / sum(jnp.sum(w, axis=0, keepdims=True) for w in weights)
        spot = lax.broadcasted_iota(jnp.int32, (block, step), 0)
        for k, w in enumerate(weights):
            share = w * scale
            hit = tail_at[:, at] - k * block == spot
            score_grad[k * block : (k + 1) * block, at] = jnp.where(hit, share - 1.0, share).astype(BF)
    tail_grad[...] = dot(score_grad[...], query[...], NN).astype(BF)


def query_grad_and_sum(relations, score_grad, tails, rows, query_grad, total):
    batches = relations.shape[0]
    edges = rows.shape[0] // batches
    query_grad[...] = dot(score_grad[...], tails[...], TN).astype(BF)
    for batch in range(batches):
        at = slice(batch * edges, (batch + 1) * edges)
        part = dot(rows[at, :], query_grad[at, :], TN)
        total[relations[batch]] += part.reshape(total.shape[1:])


def first_backward_kernel(relations, score_grad, tails, rows, query_grad, total):
    total[...] = jnp.zeros_like(total)
    query_grad_and_sum(relations, score_grad, tails, rows, query_grad, total)


def last_backward_kernel(relations, core, score_grad, tails, rows, before, query_grad, kept, sent, total):
    total[...] = before[...]
    query_grad_and_sum(relations, score_grad, tails, rows, query_grad, total)
    for r in range(total.shape[0]):
        kept[:, r] = total[r, :, core[0]]
        sent[:, r] = total[r, :, 1 - core[0]].astype(BF)


def head_kernel(relations, core, head_at, grad0, grad1, own, other, near, total, part):
    batches = relations.shape[1]
    edges = grad0.shape[0] // batches
    parts = 4
    step = total.shape[0] // parts
    first, second = halves(core[0], own.shape[2])
    for bucket, grad in enumerate((grad0, grad1)):
        for batch in range(batches):
            at = slice(batch * edges, (batch + 1) * edges)
            r = relations[bucket, batch]
            part[at, first] = dot(grad[at, :], own[r], NN).astype(BF)
            part[at, second] = dot(grad[at, :], other[r], NN).astype(BF)
        for k in range(parts):
            to = slice(k * step, (k + 1) * step)
            added = dot(picks(head_at[bucket : bucket + 1, :], k * step, step), part[...], NN)
            if bucket == 0:
                total[to, :] = added + near[to, :].astype(F32)
            else:
                total[to, :] += added


def update_kernel(far, head, table, state, new_table, new_state, held, into, out, out_done):
    parts, block = into.shape[0], state.shape[1]
    step = table.shape[0] // parts
    spans = [pl.ds(part * step, step) for part in range(parts)]
    coming = [pltpu.make_async_copy(far.at[to], held.at[to], into.at[part]) for part, to in enumerate(spans)]
    leaving = [pltpu.make_async_copy(out.at[to], new_table.at[to], out_done.at[part]) for part, to in enumerate(spans)]
    for copy in coming:
        copy.start()
    for part in range(parts):
        coming[part].wait()
        for first in range(part * step, (part + 1) * step, block):
            at, row = slice(first, first + block), slice(first // block, first // block + 1)
            grad = head[at, :] + held[at, :].astype(F32)
            before = jnp.broadcast_to(state[row, :], (block, block)).T[:, :1]
            sums = before + jnp.mean(grad * grad, axis=1, keepdims=True)
            new_state[row, :] = jnp.broadcast_to(sums, (block, block)).T[:1, :]
            out[at, :] = table[at, :] - grad * (LEARN_RATE / jnp.sqrt(sums))
        leaving[part].start()
    for copy in leaving:
        copy.wait()


def updated(head, far, table, state):
    count, width = table.shape
    block, parts = 128, UPDATE_PARTS
    anywhere = pl.BlockSpec(memory_space=pl.ANY)
    new_table, new_state = pl.pallas_call(
        update_kernel,
        out_shape=(
            jax.ShapeDtypeStruct(table.shape, F32),
            jax.ShapeDtypeStruct((count // block, block), F32),
        ),
        in_specs=[anywhere] + vmem(3),
        out_specs=(anywhere, vmem(1)[0]),
        scratch_shapes=[
            pltpu.VMEM((count, width), BF),
            pltpu.SemaphoreType.DMA((parts,)),
            pltpu.VMEM((count, width), F32),
            pltpu.SemaphoreType.DMA((parts,)),
        ],
        compiler_params=pltpu.CompilerParams(vmem_limit_bytes=VMEM_BYTES),
        cost_estimate=pl.CostEstimate(flops=8 * table.size, bytes_accessed=16 * table.size, transcendentals=0),
        name="update",
    )(far, head, table, state.reshape(count // block, block))
    return new_table, new_state.reshape(count)


def op_update_kernel(got, state, operators, new_operators, new_state):
    total = got[0].astype(F32)
    for source in range(1, got.shape[0]):
        total += got[source].astype(F32)
    columns = state.shape[2]
    for r in range(state.shape[0]):
        grad = total[:, r * columns : (r + 1) * columns]
        sums = state[r] + grad * grad
        new_state[r] = sums
        new_operators[r] = operators[r] - LEARN_RATE * grad / jnp.sqrt(sums)


def summed_over_devices(kept, sent):
    _, nrel, columns, width = kept.shape
    narrow = lax.axis_size("narrow")
    pair = (kept + swapped(sent, "wide", 0).astype(F32)).astype(BF)
    groups = strided_groups(lax.axis_size("wide"), 2)
    got = lax.all_to_all(pair, "wide", 0, 0, axis_index_groups=groups)
    part = jnp.sum(got.astype(F32), axis=0).reshape(nrel * columns, width).T
    part = part.astype(BF).reshape(narrow, width // narrow, nrel * columns)
    return lax.all_to_all(part, "narrow", 0, 0)


def step(entity_table, row_state, operators, op_state, head_index, tail_index, batch_relation):
    nrel, _, width = operators.shape
    count, edges = entity_table.shape[0], head_index.shape[1]
    narrow_count = lax.axis_size("narrow")
    wide_count = lax.axis_size("wide")
    flips = (0, narrow_count.bit_length() - 2)
    core = (lax.axis_index("wide") % 2).astype(jnp.int32).reshape(1)
    table_bf = entity_table.astype(BF)
    half = own_half_of_operators(operators)
    tails = [None, None]
    for bucket in (1, 0):
        tails[bucket] = swapped(table_bf, "narrow", flips[bucket])
    other = swapped(half, "wide", 0)
    flat = ((edges, width), BF)
    matmul = 2 * count * edges * width
    rows = local(rows_kernel, 2 * matmul, (flat, flat), (), (head_index, table_bf))
    score_grads, returned, query_grads = [None, None], [None, None], [None, None]
    for bucket in (0, 1):
        (query,) = local(
            query_kernel, matmul // 2, (flat,), (batch_relation[bucket], core), (rows[bucket], half, other)
        )
        score_grads[bucket], tail_grad = local(
            score_kernel,
            4 * matmul,
            (((count, edges), BF), ((count, width), BF)),
            (),
            (query, tails[bucket], tail_index[bucket : bucket + 1]),
        )
        returned[bucket] = swapped(tail_grad, "narrow", flips[bucket])
    sums = (nrel, wide_count // 2, 2, width // wide_count, width)
    query_grads[0], before = local(
        first_backward_kernel,
        2 * matmul,
        (flat, (sums, F32)),
        (batch_relation[0],),
        (score_grads[0], tails[0], rows[0]),
    )
    shares = (wide_count // 2, nrel, width // wide_count, width)
    query_grads[1], kept, sent = local(
        last_backward_kernel,
        2 * matmul,
        (flat, (shares, F32), (shares, BF)),
        (batch_relation[1], core),
        (score_grads[1], tails[1], rows[1], before),
        (pltpu.VMEM(sums, F32),),
    )
    op_parts = summed_over_devices(kept, sent)
    (head_total,) = local(
        head_kernel,
        3 * matmul,
        (((count, width), F32),),
        (batch_relation, core),
        (head_index, *query_grads, half, other, returned[0]),
        (pltpu.VMEM((edges, width), BF),),
    )
    new_table, new_state = updated(head_total, returned[1], entity_table, row_state)
    columns = width // wide_count
    first_column = lax.axis_index("wide") * columns
    own_operators = lax.dynamic_slice_in_dim(operators, first_column, columns, 2)
    share = (op_state.shape, F32)
    new_operators, new_op_state = local(
        op_update_kernel, 8 * op_state.size, (share, share), (), (op_parts, op_state, own_operators)
    )
    return (new_table, new_state, new_operators, new_op_state)


def solution(mesh):
    placed = (
        P(("wide", "narrow"), None),
        P(("wide", "narrow")),
        P(None, "narrow", None),
        P(None, "narrow", "wide"),
        P(None, ("wide", "narrow")),
        P(None, ("wide", "narrow")),
        P(None, ("wide", "narrow")),
    )
    return jax.shard_map(
        step,
        mesh=mesh,
        in_specs=placed,
        out_specs=(
            P(("wide", "narrow"), None),
            P(("wide", "narrow")),
            P(None, "narrow", "wide"),
            P(None, "narrow", "wide"),
        ),
        check_vma=False,
    )
```
